32 devices in a mesh: gx: 4 (over y, x), gy: 4 (over z), ma: 2 (over core).
Axes of the slice: x: 2, y: 2, z: 4, core: 2. Of those that a mesh axis runs over, the one named last changes fastest.
Arguments:
- alpha_fields: bfloat16 [80, 2, 512, 512], P('ma', None, 'gy', 'gx'), may hold values from -6 to 6
- member_perts: bfloat16 [80, 2, 512, 512], P('ma', None, 'gy', 'gx'), may hold values from -0.625 to 0.625
- band_widths: int32 [2], replicated, may hold values from 2 to 8
- lat_index: int32 [1024], P('gy'), may hold values from 0 to 510, as said below
- lat_weight: float32 [1024], P('gy'), may hold values from 0 to 1
- lon_index: int32 [1024], P('gx'), may hold values from 0 to 511, as said below
- lon_weight: float32 [1024], P('gx'), may hold values from 0 to 1
- innovation: float32 [2, 1024, 1024], P(None, 'gy', 'gx'), may hold values from -6 to 6
- obs_weight: float32 [2, 1024, 1024], P(None, 'gy', 'gx'), may hold values from 0.1 to 1
Outputs:
- increment: float32 [2, 1024, 1024], P(None, 'gy', 'gx')
- gradient: float32 [80, 2, 512, 512], P('ma', None, 'gy', 'gx')
The draws below stay inside these ranges and needn't reach their ends.
Inputs may be any that keep to these rules, and one draw needn't show every extreme that they name: lat_index[p] is p // 2 - 1 or p // 2, clamped to 0 .. 510. lon_index[q] is q // 2 - 1 or q // 2, taken modulo 512.
All inputs are finite; a program needn't handle non-finite values.
Results may differ from the reference program's by a relative error of at most 0.0003.
Values may be sent and summed in bfloat16 or wider, within the bound.
A program may use at most 128 MiB of HBM per device.

```python
import math
import jax
import jax.numpy as jnp
from jax import lax

MEM = 80
LEV = 2
HB = 8
NCLAT = 512
NCLON = 512
NFLAT = 1024
NFLON = 1024


def draw_lat_index(key, part):
    position = jnp.arange(NFLAT, dtype=jnp.int32)
    backward = jax.random.randint(key, (NFLAT,), 0, 2, dtype=jnp.int32)
    return jnp.clip(position // 2 - backward, 0, NCLAT - 2).astype(jnp.int32)


def draw_lon_index(key, part):
    position = jnp.arange(NFLON, dtype=jnp.int32)
    backward = jax.random.randint(key, (NFLON,), 0, 2, dtype=jnp.int32)
    return jnp.remainder(position // 2 - backward, NCLON).astype(jnp.int32)


def steps_of(own_key, dims, cuts, smallest, top_value):
    def one(dim, shards_of):
        heights = jax.random.uniform(jax.random.fold_in(jax.random.fold_in(own_key, 6), dim), (shards_of,), jnp.float32, smallest / len(cuts), top_value / len(cuts))
        return jnp.repeat(jnp.exp(heights), dims[dim] // shards_of).reshape((-1,) + (1,) * (len(dims) - dim - 1))

    gain = one(*cuts[0])
    for cut in cuts[1:]:
        gain = gain * one(*cut)
    return gain


def normal_values(rng, extent, width, limit, shards=(), kind=jnp.bfloat16):
    entries = width * jax.random.normal(rng, extent, jnp.float32)
    if shards:
        entries = entries * steps_of(rng, extent, shards, -0.22, 0.18)
    return jnp.clip(entries, -limit, limit).astype(kind)


def setup_inputs(seed: int = 0) -> dict:
    splits = jax.random.split(jax.random.key(seed), 10)
    return {
        "alpha_fields": normal_values(splits[0], (MEM, LEV, NCLAT, NCLON), 1.0, 6.0, ((0, 2), (2, 4), (3, 4))),
        "member_perts": normal_values(splits[1], (MEM, LEV, NCLAT, NCLON), MEM ** -0.5, 0.625, ((0, 2), (2, 4), (3, 4))),
        "band_widths": jax.random.randint(splits[2], (LEV,), 2, HB + 1).astype(jnp.int32),
        "lat_index": draw_lat_index(jax.random.fold_in(splits[9], 71), 0),
        "lat_weight": jnp.clip(1.0 * jax.random.uniform(splits[4], (NFLAT,), jnp.float32) ** steps_of(splits[4], (NFLAT,), ((0, 4),), -0.2, 0.2), 0.0, 1.0),
        "lon_index": draw_lon_index(jax.random.fold_in(splits[9], 71), 0),
        "lon_weight": jnp.clip(1.0 * jax.random.uniform(splits[6], (NFLON,), jnp.float32) ** steps_of(splits[6], (NFLON,), ((0, 4),), -0.2, 0.2), 0.0, 1.0),
        "innovation": normal_values(splits[7], (LEV, NFLAT, NFLON), 1.0, 6.0, ((1, 4), (2, 4)), jnp.float32),
        "obs_weight": jnp.clip(jnp.exp(math.log(1.0) - 2.3025851 * jax.random.uniform(splits[8], (LEV, NFLAT, NFLON), jnp.float32) ** steps_of(splits[8], (LEV, NFLAT, NFLON), ((1, 4), (2, 4)), -0.2, 0.2)), 0.1, 1.0),
    }


def tap_table(band_widths):
    tap_offsets = jnp.arange(-HB, HB + 1).astype(jnp.float32)
    spread = band_widths.astype(jnp.float32)[:, None]
    shapes = jnp.exp(-tap_offsets[None, :] ** 2 / (2.0 * spread * spread))
    return shapes / jnp.sqrt(lax.optimization_barrier(jnp.sum(shapes * shapes, axis=1, keepdims=True)))

def localize(source, filter_taps):
    along_lon = jnp.zeros_like(source)
    for tap_number in range(2 * HB + 1):
        along_lon = along_lon + filter_taps[:, tap_number, None, None] * jnp.roll(source, HB - tap_number, axis=2)
    padded = jnp.pad(along_lon, ((0, 0), (HB, HB), (0, 0)))
    result = jnp.zeros_like(source)
    for tap_number in range(2 * HB + 1):
        result = result + filter_taps[:, tap_number, None, None] * padded[:, tap_number:tap_number + NCLAT, :]
    return result

def reference(alpha_fields, member_perts, band_widths, lat_index, lat_weight, lon_index, lon_weight, innovation, obs_weight):
    filter_taps = tap_table(band_widths)

    def accumulate(running, member_pair):
        localized = localize(member_pair[0].astype(jnp.float32), filter_taps)
        return (running + member_pair[1].astype(jnp.float32) * localized, None)
    coarse_increment, unused = lax.scan(accumulate, jnp.zeros((LEV, NCLAT, NCLON), jnp.float32), (alpha_fields, member_perts))
    lat_next = (lat_index + 1).astype(jnp.int32)
    lon_next = jnp.remainder(lon_index + 1, NCLON).astype(jnp.int32)
    north_weight = lat_weight[None, :, None]
    east_weight = lon_weight[None, None, :]
    by_lat = (1.0 - north_weight) * coarse_increment[:, lat_index, :] + north_weight * coarse_increment[:, lat_next, :]
    increment = (1.0 - east_weight) * by_lat[:, :, lon_index] + east_weight * by_lat[:, :, lon_next]
    misfit = obs_weight * (increment - innovation)
    spread_lon = jnp.zeros((LEV, NFLAT, NCLON), jnp.float32)
    spread_lon = spread_lon.at[:, :, lon_index].add((1.0 - east_weight) * misfit)
    spread_lon = spread_lon.at[:, :, lon_next].add(east_weight * misfit)
    coarse_residual = jnp.zeros((LEV, NCLAT, NCLON), jnp.float32)
    coarse_residual = coarse_residual.at[:, lat_index, :].add((1.0 - north_weight) * spread_lon)
    coarse_residual = coarse_residual.at[:, lat_next, :].add(north_weight * spread_lon)

    def member_gradient(member_pair):
        product = member_pair[1].astype(jnp.float32) * coarse_residual
        return member_pair[0].astype(jnp.float32) + localize(product, filter_taps)
    gradient = lax.map(member_gradient, (alpha_fields, member_perts))
    return (increment, gradient)
```

```python
import jax
import jax.numpy as jnp
from jax import lax
from jax.experimental import pallas as pl
from jax.experimental.pallas import tpu as pltpu
from jax.sharding import PartitionSpec as P

HB = 8
GROUP = 8
CH = HB + 2
FH = 2 * HB + 2
HIGHEST = lax.Precision.HIGHEST
F32 = jnp.float32
BF16 = jnp.bfloat16


def shifts(axis, periodic):
    count = lax.axis_size(axis)
    forward = [(i, i + 1) for i in range(count - 1)]
    if periodic:
        forward.append((count - 1, 0))
    return forward, [(target, source) for source, target in forward]


def swap_edges(low_edge, high_edge, axis, periodic):
    forward, backward = shifts(axis, periodic)
    return (
        lax.ppermute(high_edge, axis, forward),
        lax.ppermute(low_edge, axis, backward),
    )


def framed(block, axis, dim, width, periodic):
    size = block.shape[dim]
    low, high = swap_edges(
        lax.slice_in_dim(block, 0, width, axis=dim),
        lax.slice_in_dim(block, size - width, size, axis=dim),
        axis,
        periodic,
    )
    return jnp.concatenate([block, low, high], axis=dim)


def place(order, size, width):
    return jnp.where(order < size, order, jnp.where(order < size + width, order - size - width, order - width))


def tap_value(distance, spread, scale):
    d = distance.astype(F32)
    return jnp.where(jnp.abs(distance) <= HB, jnp.exp(-(d * d) / (2.0 * spread * spread)) * scale, 0.0)


def split_cols(value, column, half):
    high = lax.reduce_precision(value, 8, 7)
    return jnp.where(column < half, high, value - high).astype(BF16)


def filter_matrices(band_widths, rows, cols):
    levels = band_widths.shape[0]
    spread = band_widths.astype(F32)
    offsets = jnp.arange(-HB, HB + 1).astype(F32)
    shapes = jnp.exp(-(offsets[None, :] ** 2) / (2.0 * spread[:, None] * spread[:, None]))
    scale = 1.0 / jnp.sqrt(jnp.sum(shapes * shapes, axis=1))
    half = GROUP * HB
    shape = (levels, GROUP, cols + 2 * half, 2 * cols)
    l = lax.broadcasted_iota(jnp.int32, shape, 0)
    k = lax.broadcasted_iota(jnp.int32, shape, 1)
    r = lax.broadcasted_iota(jnp.int32, shape, 2)
    c = lax.broadcasted_iota(jnp.int32, shape, 3)
    q = r - cols
    west = (q // half) == l
    pos = jnp.where(r < cols, r, jnp.where(west, q % HB - HB, cols + q % HB))
    valid = (r < cols) | ((q % half) // HB == k)
    dist = jnp.where(valid, pos - c % cols, 2 * HB)
    lon = split_cols(tap_value(dist, spread[:, None, None, None], scale[:, None, None, None]), c, cols)
    shape = (levels, 2 * rows, rows + 2 * HB)
    i = lax.broadcasted_iota(jnp.int32, shape, 1)
    r = lax.broadcasted_iota(jnp.int32, shape, 2)
    dist = place(r, rows, HB) - i % rows
    lat = split_cols(tap_value(dist, spread[:, None, None], scale[:, None, None]), i, rows)
    return lon, lat


def dot(a, b):
    return jnp.dot(a, b, preferred_element_type=F32)


def rows16(north, south):
    return jnp.concatenate([north.astype(F32), south.astype(F32)], axis=0)


def pack_kernel(core, north, south, right, left, pick):
    cols = core.shape[3]
    half = GROUP * HB
    levels = core.shape[1]

    @pl.when(pl.program_id(0) == 0)
    def _():
        r = lax.broadcasted_iota(jnp.int32, (cols, 4 * half), 0)
        c = lax.broadcasted_iota(jnp.int32, (cols, 4 * half), 1)
        for l in range(levels):
            for k in range(GROUP):
                to_right = c - (l * half + HB * k)
                to_left = c - 2 * half - ((1 - l) * half + HB * k)
                hit = ((to_right >= 0) & (to_right < HB) & (r == cols - HB + to_right)) | (
                    (to_left >= 0) & (to_left < HB) & (r == to_left)
                )
                pick[l * GROUP + k] = jnp.where(hit, 1.0, 0.0).astype(BF16)

    total = None
    for l in range(levels):
        for k in range(GROUP):
            edge = rows16(north[k, l], south[k, l]).astype(BF16)
            part = dot(jnp.concatenate([core[k, l], edge], axis=0), pick[l * GROUP + k])
            total = part if total is None else total + part
    right[0] = total[:, : 2 * half].astype(BF16)
    left[0] = total[:, 2 * half :].astype(BF16)


def cost(flops, nbytes):
    return pl.CostEstimate(flops=flops, bytes_accessed=nbytes, transcendentals=0)


def pack(field, north, south):
    members, levels, rows, cols = field.shape
    steps = members // GROUP
    tall = rows + 2 * HB
    wide = 2 * GROUP * HB
    strip = pl.BlockSpec((GROUP, levels, HB, cols), lambda g: (g, 0, 0, 0))
    out = pl.BlockSpec((1, tall, wide), lambda g: (g, 0, 0))
    return pl.pallas_call(
        pack_kernel,
        grid=(steps,),
        in_specs=[pl.BlockSpec((GROUP, levels, rows, cols), lambda g: (g, 0, 0, 0)), strip, strip],
        out_specs=[out, out],
        out_shape=[jax.ShapeDtypeStruct((steps, tall, wide), BF16)] * 2,
        scratch_shapes=[pltpu.VMEM((levels * GROUP, cols, 2 * wide), BF16)],
        cost_estimate=cost(members * levels * tall * cols * wide * 4, field.size * 2),
    )(field, north, south)


def merged(west, east, level):
    lane = lax.broadcasted_iota(jnp.int32, west.shape, 1)
    w, e = west.astype(F32), east.astype(F32)
    a, b = (w, e) if level == 0 else (e, w)
    return jnp.where(lane < GROUP * HB, a, b)


def split(value):
    high = value.astype(BF16)
    return high, (value - high.astype(F32)).astype(BF16)


def lat_stage(u, lat_l):
    rows = lat_l.shape[0] // 2
    high, low = split(u)
    both = dot(lat_l, high)
    return both[:rows] + both[rows:] + dot(lat_l[:rows], low)


def forward_kernel(alpha, north, south, west, east, perts, lon, lat, out):
    cols = alpha.shape[3]

    @pl.when(pl.program_id(0) == 0)
    def _():
        out[...] = jnp.zeros_like(out)

    for l in range(alpha.shape[1]):
        side = merged(west[0], east[0], l).astype(BF16)
        total = None
        for k in range(GROUP):
            edge = rows16(north[k, l], south[k, l]).astype(BF16)
            tall = jnp.concatenate([alpha[k, l], edge], axis=0)
            both = dot(jnp.concatenate([tall, side], axis=1), lon[l, k])
            v = lat_stage(both[:, :cols] + both[:, cols:], lat[l])
            part = perts[k, l].astype(F32) * v
            total = part if total is None else total + part
        out[l] += total


def adjoint_kernel(alpha, perts, north, south, west, east, residual, lon, lat, out):
    cols = alpha.shape[3]
    rows = alpha.shape[2]
    for l in range(alpha.shape[1]):
        res = residual[l, :, :cols]
        side_h, side_l = split(merged(west[0], east[0], l) * residual[l, :, cols:])
        for k in range(GROUP):
            prod = jnp.concatenate(
                [
                    perts[k, l].astype(F32) * res[:rows],
                    rows16(north[k, l], south[k, l]) * res[rows:],
                ],
                axis=0,
            )
            high, low = split(prod)
            both = dot(jnp.concatenate([high, side_h], axis=1), lon[l, k])
            u = both[:, :cols] + both[:, cols:]
            u = u + dot(jnp.concatenate([low, side_l], axis=1), lon[l, k, :, :cols])
            out[k, l] = alpha[k, l].astype(F32) + lat_stage(u, lat[l])


def specs(alpha, lon, lat):
    members, levels, rows, cols = alpha.shape
    block = pl.BlockSpec((GROUP, levels, rows, cols), lambda g: (g, 0, 0, 0))
    strip = pl.BlockSpec((GROUP, levels, HB, cols), lambda g: (g, 0, 0, 0))
    side = pl.BlockSpec((1, rows + 2 * HB, 2 * GROUP * HB), lambda g: (g, 0, 0))
    lon_spec = pl.BlockSpec(lon.shape, lambda g: (0, 0, 0, 0))
    lat_spec = pl.BlockSpec(lat.shape, lambda g: (0, 0, 0))
    return block, strip, side, lon_spec, lat_spec


def forward(alpha, north, south, west, east, perts, lon, lat):
    members, levels, rows, cols = alpha.shape
    block, strip, side, lon_spec, lat_spec = specs(alpha, lon, lat)
    return pl.pallas_call(
        forward_kernel,
        grid=(members // GROUP,),
        in_specs=[block, strip, strip, side, side, block, lon_spec, lat_spec],
        out_specs=pl.BlockSpec((levels, rows, cols), lambda g: (0, 0, 0)),
        out_shape=jax.ShapeDtypeStruct((levels, rows, cols), F32),
        cost_estimate=cost(members * levels * 2**25, alpha.size * 4),
    )(alpha, north, south, west, east, perts, lon, lat)


def adjoint(alpha, perts, north, south, west, east, residual, lon, lat):
    members, levels, rows, cols = alpha.shape
    block, strip, side, lon_spec, lat_spec = specs(alpha, lon, lat)
    return pl.pallas_call(
        adjoint_kernel,
        grid=(members // GROUP,),
        in_specs=[
            block,
            block,
            strip,
            strip,
            side,
            side,
            pl.BlockSpec(residual.shape, lambda g: (0, 0, 0)),
            lon_spec,
            lat_spec,
        ],
        out_specs=block,
        out_shape=jax.ShapeDtypeStruct(alpha.shape, F32),
        cost_estimate=cost(members * levels * 2**25, alpha.size * 8),
    )(alpha, perts, north, south, west, east, residual, lon, lat)


def exact_dot(a, b):
    return jnp.dot(a, b, preferred_element_type=F32, precision=HIGHEST)


def weigh(cell, index, weight):
    return jnp.where(cell == index, 1.0 - weight, 0.0) + jnp.where(cell == index + 1, weight, 0.0)


def fine_kernel(coarse, fine, lat_col, lat_row, lon_col, lon_row, increment, residual):
    levels, rows, cols = coarse.shape[0], coarse.shape[1] - 2 * CH, coarse.shape[2] - 2 * CH
    tall, wide = fine.shape[2], fine.shape[3]
    half = GROUP * HB

    def iota(shape, dim):
        return lax.broadcasted_iota(jnp.int32, shape, dim)

    def col(ref):
        return ref[:, 0:1].astype(jnp.int32), ref[:, 1:2]

    def row(ref):
        return ref[0:1, :].astype(jnp.int32), ref[1:2, :]

    up_lat = weigh(place(iota((tall, rows + 2 * CH), 1), rows, CH), *col(lat_col))
    up_lon = weigh(place(iota((cols + 2 * CH, wide), 0), cols, CH), *row(lon_row))
    down_lat = weigh(place(iota((rows + 2 * HB, tall), 0), rows, HB), *row(lat_row))
    order = iota((wide, cols + 2 * half), 1)
    q = order - cols
    for l in range(levels):
        inc = exact_dot(exact_dot(up_lat, coarse[l]), up_lon)
        increment[l] = inc[: increment.shape[1], : increment.shape[2]]
        misfit = fine[1, l] * (inc - fine[0, l])
        west = (q // half) == l
        pos = jnp.where(order < cols, order, jnp.where(west, q % HB - HB, cols + q % HB))
        down_lon = weigh(pos, *col(lon_col))
        residual[l] = exact_dot(down_lat, exact_dot(misfit, down_lon))


def fine_step(coarse, fine, lat_data, lon_data, rows, cols, fine_rows, fine_cols):
    levels = coarse.shape[0]
    return pl.pallas_call(
        fine_kernel,
        out_shape=[
            jax.ShapeDtypeStruct((levels, fine_rows, fine_cols), F32),
            jax.ShapeDtypeStruct((levels, rows + 2 * HB, cols + 2 * GROUP * HB), F32),
        ],
        cost_estimate=cost(2**29, 2**21),
    )(coarse, fine, lat_data.T, lat_data, lon_data.T, lon_data)


def halo_fields(field):
    rows = field.shape[2]
    north, south = swap_edges(field[:, :, :HB], field[:, :, rows - HB :], "gy", False)
    right, left = pack(field, north, south)
    west, east = swap_edges(left, right, "gx", True)
    return north, south, west, east


def body(
    alpha_fields,
    member_perts,
    band_widths,
    lat_index,
    lat_weight,
    lon_index,
    lon_weight,
    innovation,
    obs_weight,
):
    rows, cols = alpha_fields.shape[2:]
    lon, lat = filter_matrices(band_widths, rows, cols)
    a_north, a_south, a_west, a_east = halo_fields(alpha_fields)
    p_north, p_south, p_west, p_east = halo_fields(member_perts)

    fine = jnp.stack([innovation, obs_weight])
    fine = framed(framed(fine, "gy", 2, FH, False), "gx", 3, FH, True)
    lat_start = lax.axis_index("gy") * rows
    lon_start = lax.axis_index("gx") * cols
    lon_total = cols * lax.axis_size("gx")
    lat_data = framed(jnp.stack([lat_index.astype(F32), lat_weight]), "gy", 1, FH, False)
    lon_data = framed(jnp.stack([lon_index.astype(F32), lon_weight]), "gx", 1, FH, True)
    lat_rel = lat_data[0] - lat_start.astype(F32)
    lon_rel = (
        jnp.remainder(lon_data[0].astype(jnp.int32) - lon_start + CH, lon_total) - CH
    ).astype(F32)
    lat_data = jnp.stack([lat_rel, lat_data[1]])
    lon_data = jnp.stack([lon_rel, lon_data[1]])

    partial = forward(alpha_fields, a_north, a_south, a_west, a_east, member_perts, lon, lat)
    count = lax.axis_size("ma")
    total = partial
    moving = partial
    for _ in range(count - 1):
        moving = lax.ppermute(moving, "ma", [(i, (i + 1) % count) for i in range(count)])
        total = total + moving
    coarse = framed(framed(total, "gx", 2, CH, True), "gy", 1, CH, False)
    increment, residual = fine_step(
        coarse, fine, lat_data, lon_data, rows, cols, innovation.shape[1], innovation.shape[2]
    )
    gradient = adjoint(
        alpha_fields, member_perts, p_north, p_south, p_west, p_east, residual, lon, lat
    )
    return (increment, gradient)


def solution(mesh):
    placed = (
        P("ma", None, "gy", "gx"),
        P("ma", None, "gy", "gx"),
        P(),
        P("gy"),
        P("gy"),
        P("gx"),
        P("gx"),
        P(None, "gy", "gx"),
        P(None, "gy", "gx"),
    )
    return jax.shard_map(
        body,
        mesh=mesh,
        in_specs=placed,
        out_specs=(P(None, "gy", "gx"), P("ma", None, "gy", "gx")),
        check_vma=False,
    )
```

```python
import jax
import jax.numpy as jnp
from jax import lax
from jax.experimental import pallas as pl
from jax.experimental.pallas import tpu as pltpu
from jax.sharding import PartitionSpec as P

HB = 8
GROUP = 8
FR = 24
FC = 32
CR = 16
MESH = pl.DeviceIdType.MESH
VMEM_LIMIT = 60 * 2**20
HIGHEST = lax.Precision.HIGHEST
F32 = jnp.float32
BF16 = jnp.bfloat16


def place(order, size, width):
    return jnp.where(order < size, order, jnp.where(order < size + width, order - size - width, order - width))


def tap_value(distance, spread, scale):
    d = distance.astype(F32)
    return jnp.where(jnp.abs(distance) <= HB, jnp.exp(-(d * d) / (2.0 * spread * spread)) * scale, 0.0)


def split_cols(value, column, half):
    high = lax.reduce_precision(value, 8, 7)
    return jnp.where(column < half, high, value - high).astype(BF16)


def filter_matrices(band_widths, rows, cols):
    levels = band_widths.shape[0]
    spread = band_widths.astype(F32)
    offsets = jnp.arange(-HB, HB + 1).astype(F32)
    shapes = jnp.exp(-(offsets[None, :] ** 2) / (2.0 * spread[:, None] * spread[:, None]))
    scale = 1.0 / jnp.sqrt(jnp.sum(shapes * shapes, axis=1))
    half = GROUP * HB
    shape = (levels, GROUP, cols + 2 * half, 2 * cols)
    l = lax.broadcasted_iota(jnp.int32, shape, 0)
    k = lax.broadcasted_iota(jnp.int32, shape, 1)
    r = lax.broadcasted_iota(jnp.int32, shape, 2)
    c = lax.broadcasted_iota(jnp.int32, shape, 3)
    q = r - cols
    west = (q // half) == l
    pos = jnp.where(r < cols, r, jnp.where(west, q % HB - HB, cols + q % HB))
    valid = (r < cols) | ((q % half) // HB == k)
    dist = jnp.where(valid, pos - c % cols, 2 * HB)
    lon = split_cols(tap_value(dist, spread[:, None, None, None], scale[:, None, None, None]), c, cols)
    shape = (levels, 2 * rows, rows + 2 * HB)
    i = lax.broadcasted_iota(jnp.int32, shape, 1)
    r = lax.broadcasted_iota(jnp.int32, shape, 2)
    dist = place(r, rows, HB) - i % rows
    lat = split_cols(tap_value(dist, spread[:, None, None], scale[:, None, None]), i, rows)
    return lon, lat


def dot(a, b):
    return jnp.dot(a, b, preferred_element_type=F32)


def rows16(north, south):
    return jnp.concatenate([north.astype(F32), south.astype(F32)], axis=0)


class Link:
    def __init__(self, axis, step, src, dst, send, recv, slot, periodic):
        me, count = lax.axis_index(axis), lax.axis_size(axis)
        target = me + step
        self.sends = self.gets = None
        if periodic:
            target = lax.rem(target + count, count)
        else:
            self.sends = (target >= 0) & (target < count)
            self.gets = (me - step >= 0) & (me - step < count)
        self.dst = dst
        self.copy = pltpu.make_async_remote_copy(
            src_ref=src,
            dst_ref=dst,
            send_sem=send.at[slot],
            recv_sem=recv.at[slot],
            device_id={axis: target},
            device_id_type=MESH,
        )

    def start(self):
        if self.sends is None:
            self.copy.start()
        else:
            pl.when(self.sends)(self.copy.start)

    def arrive(self):
        if self.gets is None:
            self.copy.wait_recv()
        else:
            pl.when(self.gets)(self.copy.wait_recv)

            @pl.when(jnp.logical_not(self.gets))
            def _():
                self.dst[...] = jnp.zeros_like(self.dst)

    def sent(self):
        if self.sends is None:
            self.copy.wait_send()
        else:
            pl.when(self.sends)(self.copy.wait_send)


def greet(others):
    barrier = pltpu.get_barrier_semaphore()
    gx, gxn = lax.axis_index("gx"), lax.axis_size("gx")
    gy, gyn = lax.axis_index("gy"), lax.axis_size("gy")
    for step in (1, gxn - 1):
        pl.semaphore_signal(
            barrier, inc=1, device_id={"gx": lax.rem(gx + step, gxn)}, device_id_type=MESH
        )
    for peer in others:
        pl.semaphore_signal(barrier, inc=1, device_id={"ma": peer}, device_id_type=MESH)
    for step, there in ((-1, gy > 0), (1, gy < gyn - 1)):

        @pl.when(there)
        def _(step=step):
            pl.semaphore_signal(barrier, inc=1, device_id={"gy": gy + step}, device_id_type=MESH)

    below, above = jnp.minimum(gy, 1), jnp.minimum(gyn - 1 - gy, 1)
    pl.semaphore_wait(barrier, 2 + len(others) + below + above)


def exchange_kernel(
    alpha, perts, innov, weight, lat, lon,
    a_north, a_south, a_west, a_east, p_north, p_south, p_west, p_east,
    fine_low, fine_high, fine_west, fine_east, lat_low, lat_high, lon_west, lon_east,
    a_tile, p_tile, fine_tile, pick, a_right, a_left, p_right, p_left, f_right, f_left,
    send, recv, local,
):
    members, levels, rows, cols = alpha.shape
    half = GROUP * HB
    frows, fcols = innov.shape[1:]
    loads = [
        pltpu.make_async_copy(src, dst, local.at[i])
        for i, (src, dst) in enumerate(
            ((alpha, a_tile), (perts, p_tile), (innov, fine_tile.at[0]), (weight, fine_tile.at[1]))
        )
    ]
    for load in loads:
        load.start()
    greet(())
    slots = iter(range(64))

    def link(axis, step, src, dst):
        return Link(axis, step, src, dst, send, recv, next(slots), axis == "gx")

    a_rows = [
        link("gy", 1, alpha.at[:, :, pl.ds(rows - HB, HB), :], a_north),
        link("gy", -1, alpha.at[:, :, pl.ds(0, HB), :], a_south),
    ]
    f_rows = [
        link("gy", 1, innov.at[:, pl.ds(frows - FR, FR), :], fine_low.at[0]),
        link("gy", -1, innov.at[:, pl.ds(0, FR), :], fine_high.at[0]),
        link("gy", 1, weight.at[:, pl.ds(frows - FR, FR), :], fine_low.at[1]),
        link("gy", -1, weight.at[:, pl.ds(0, FR), :], fine_high.at[1]),
    ]
    p_rows = [
        link("gy", 1, perts.at[:, :, pl.ds(rows - HB, HB), :], p_north),
        link("gy", -1, perts.at[:, :, pl.ds(0, HB), :], p_south),
    ]
    small = [
        link("gy", 1, lat, lat_low),
        link("gy", -1, lat, lat_high),
        link("gx", 1, lon, lon_west),
        link("gx", -1, lon, lon_east),
    ]
    for one in a_rows + f_rows + p_rows + small:
        one.start()

    r = lax.broadcasted_iota(jnp.int32, (cols, 4 * half), 0)
    c = lax.broadcasted_iota(jnp.int32, (cols, 4 * half), 1)
    for l in range(levels):
        for k in range(GROUP):
            to_right = c - (l * half + HB * k)
            to_left = c - 2 * half - ((1 - l) * half + HB * k)
            hit = ((to_right >= 0) & (to_right < HB) & (r == cols - HB + to_right)) | (
                (to_left >= 0) & (to_left < HB) & (r == to_left)
            )
            pick[l * GROUP + k] = jnp.where(hit, 1.0, 0.0).astype(BF16)

    def packed(first, count, right, left, piece):
        @pl.loop(0, members // GROUP)
        def _(g):
            total = None
            for l in range(levels):
                for k in range(GROUP):
                    part = dot(piece(g * GROUP + k, l), pick[l * GROUP + k])
                    total = part if total is None else total + part
            right[g, first : first + count] = total[:, : 2 * half].astype(BF16)
            left[g, first : first + count] = total[:, 2 * half :].astype(BF16)

    def sides(first, count, right, left, west, east):
        span = pl.ds(first, count)
        pair = [
            link("gx", 1, right.at[:, span, :], west.at[:, span, :]),
            link("gx", -1, left.at[:, span, :], east.at[:, span, :]),
        ]
        for one in pair:
            one.start()
        return pair

    flying = []
    fields = (
        (a_tile, loads[0], a_rows, a_north, a_south, a_right, a_left, a_west, a_east),
        (p_tile, loads[1], p_rows, p_north, p_south, p_right, p_left, p_west, p_east),
    )
    for tile, load, _, _, _, right, left, west, east in fields:
        load.wait()
        packed(0, rows, right, left, lambda m, l: tile[m, l])
        flying += sides(0, rows, right, left, west, east)
    for _, _, arrivals, north, south, right, left, west, east in fields:
        for one in arrivals:
            one.arrive()
        packed(
            rows, 2 * HB, right, left, lambda m, l: rows16(north[m, l], south[m, l]).astype(BF16)
        )
        flying += sides(rows, 2 * HB, right, left, west, east)
    loads[2].wait()
    loads[3].wait()
    for one in f_rows:
        one.arrive()

    def edge_of(part, start):
        return jnp.concatenate(
            [part[i, l, :, start : start + FC] for i in range(2) for l in range(levels)], axis=1
        )

    for first, part in ((0, fine_tile), (frows, fine_low), (frows + FR, fine_high)):
        count = part.shape[2]
        f_right[first : first + count] = edge_of(part, fcols - FC)
        f_left[first : first + count] = edge_of(part, 0)
    f_sides = [link("gx", 1, f_right, fine_west), link("gx", -1, f_left, fine_east)]
    for one in f_sides:
        one.start()
    for one in flying + f_sides + small:
        one.arrive()
    for one in a_rows + f_rows + p_rows + flying + f_sides + small:
        one.sent()


def cost(flops, nbytes):
    return pl.CostEstimate(flops=flops, bytes_accessed=nbytes, transcendentals=0)


def exchange(alpha, perts, innov, weight, lat, lon):
    members, levels, rows, cols = alpha.shape
    steps, tall, wide = members // GROUP, rows + 2 * HB, 2 * GROUP * HB
    frows, fcols = innov.shape[1:]
    strip = (members, levels, HB, cols)
    side = (steps, tall, wide)
    fine_rows = (2, levels, FR, fcols)
    fine_side = (frows + 2 * FR, 2 * levels * FC)
    outs = [(strip, BF16)] * 2 + [(side, BF16)] * 2
    outs = outs + outs + [(fine_rows, F32)] * 2 + [(fine_side, F32)] * 2
    outs = outs + [(lat.shape, F32)] * 2 + [(lon.shape, F32)] * 2
    vmem = pl.BlockSpec(memory_space=pltpu.VMEM)
    anywhere = pl.BlockSpec(memory_space=pl.ANY)
    return pl.pallas_call(
        exchange_kernel,
        in_specs=[anywhere] * 4 + [vmem] * 2,
        out_specs=[vmem] * len(outs),
        out_shape=[jax.ShapeDtypeStruct(shape, kind) for shape, kind in outs],
        scratch_shapes=[
            pltpu.VMEM(alpha.shape, BF16),
            pltpu.VMEM(alpha.shape, BF16),
            pltpu.VMEM((2,) + innov.shape, F32),
            pltpu.VMEM((levels * GROUP, cols, 2 * wide), BF16),
        ]
        + [pltpu.VMEM(side, BF16)] * 4
        + [pltpu.VMEM(fine_side, F32)] * 2
        + [
            pltpu.SemaphoreType.DMA((24,)),
            pltpu.SemaphoreType.DMA((24,)),
            pltpu.SemaphoreType.DMA((4,)),
        ],
        compiler_params=pltpu.CompilerParams(
            collective_id=0, has_side_effects=True, vmem_limit_bytes=VMEM_LIMIT
        ),
        cost_estimate=cost(2**30, 2**24),
    )(alpha, perts, innov, weight, lat, lon)


def merged(west, east, level):
    lane = lax.broadcasted_iota(jnp.int32, west.shape, 1)
    w, e = west.astype(F32), east.astype(F32)
    a, b = (w, e) if level == 0 else (e, w)
    return jnp.where(lane < GROUP * HB, a, b)


def split(value):
    high = value.astype(BF16)
    return high, (value - high.astype(F32)).astype(BF16)


def lat_stage(u, lat_l):
    rows = lat_l.shape[0] // 2
    high, low = split(u)
    both = dot(lat_l, high)
    return both[:rows] + both[rows:] + dot(lat_l[:rows], low)


def forward_kernel(alpha, north, south, west, east, perts, lon, lat, out):
    cols = alpha.shape[3]

    @pl.when(pl.program_id(0) == 0)
    def _():
        out[...] = jnp.zeros_like(out)

    for l in range(alpha.shape[1]):
        side = merged(west[0], east[0], l).astype(BF16)
        total = None
        for k in range(GROUP):
            edge = rows16(north[k, l], south[k, l]).astype(BF16)
            tall = jnp.concatenate([alpha[k, l], edge], axis=0)
            both = dot(jnp.concatenate([tall, side], axis=1), lon[l, k])
            v = lat_stage(both[:, :cols] + both[:, cols:], lat[l])
            part = perts[k, l].astype(F32) * v
            total = part if total is None else total + part
        out[l] += total


def adjoint_kernel(alpha, perts, north, south, west, east, residual, lon, lat, out):
    cols = alpha.shape[3]
    rows = alpha.shape[2]
    for l in range(alpha.shape[1]):
        res = residual[l, :, :cols]
        side_h, side_l = split(merged(west[0], east[0], l) * residual[l, :, cols:])
        for k in range(GROUP):
            prod = jnp.concatenate(
                [
                    perts[k, l].astype(F32) * res[:rows],
                    rows16(north[k, l], south[k, l]) * res[rows:],
                ],
                axis=0,
            )
            high, low = split(prod)
            both = dot(jnp.concatenate([high, side_h], axis=1), lon[l, k])
            u = both[:, :cols] + both[:, cols:]
            u = u + dot(jnp.concatenate([low, side_l], axis=1), lon[l, k, :, :cols])
            out[k, l] = alpha[k, l].astype(F32) + lat_stage(u, lat[l])


def specs(alpha, lon, lat):
    members, levels, rows, cols = alpha.shape
    block = pl.BlockSpec((GROUP, levels, rows, cols), lambda g: (g, 0, 0, 0))
    strip = pl.BlockSpec((GROUP, levels, HB, cols), lambda g: (g, 0, 0, 0))
    side = pl.BlockSpec((1, rows + 2 * HB, 2 * GROUP * HB), lambda g: (g, 0, 0))
    lon_spec = pl.BlockSpec(lon.shape, lambda g: (0, 0, 0, 0))
    lat_spec = pl.BlockSpec(lat.shape, lambda g: (0, 0, 0))
    return block, strip, side, lon_spec, lat_spec


def forward(alpha, north, south, west, east, perts, lon, lat):
    members, levels, rows, cols = alpha.shape
    block, strip, side, lon_spec, lat_spec = specs(alpha, lon, lat)
    return pl.pallas_call(
        forward_kernel,
        grid=(members // GROUP,),
        in_specs=[block, strip, strip, side, side, block, lon_spec, lat_spec],
        out_specs=pl.BlockSpec((levels, rows, cols), lambda g: (0, 0, 0)),
        out_shape=jax.ShapeDtypeStruct((levels, rows, cols), F32),
        cost_estimate=cost(members * levels * 2**25, alpha.size * 4),
    )(alpha, north, south, west, east, perts, lon, lat)


def adjoint(alpha, perts, north, south, west, east, residual, lon, lat):
    members, levels, rows, cols = alpha.shape
    block, strip, side, lon_spec, lat_spec = specs(alpha, lon, lat)
    return pl.pallas_call(
        adjoint_kernel,
        grid=(members // GROUP,),
        in_specs=[
            block,
            block,
            strip,
            strip,
            side,
            side,
            pl.BlockSpec(residual.shape, lambda g: (0, 0, 0)),
            lon_spec,
            lat_spec,
        ],
        out_specs=block,
        out_shape=jax.ShapeDtypeStruct(alpha.shape, F32),
        cost_estimate=cost(members * levels * 2**25, alpha.size * 8),
    )(alpha, perts, north, south, west, east, residual, lon, lat)


def exact_dot(a, b):
    return jnp.dot(a, b, preferred_element_type=F32, precision=HIGHEST)


def across(a, b, dims):
    return lax.dot_general(
        a, b, ((dims[:1], dims[1:]), ((), ())), precision=HIGHEST, preferred_element_type=F32
    )


def weigh(cell, index, weight):
    cell = cell.astype(F32)
    return jnp.where(cell == index, 1.0 - weight, 0.0) + jnp.where(cell == index + 1.0, weight, 0.0)


def fine_kernel(
    partial, innov, weight, fine_low, fine_high, fine_west, fine_east,
    lat, lat_low, lat_high, lon, lon_west, lon_east,
    increment, residual,
    mine, other, cells, edge, low, high, send, recv,
):
    levels, rows, cols = partial.shape
    frows, fcols = innov.shape[1:]
    tall, wide = frows + 2 * FR, fcols + 2 * FC
    half = GROUP * HB
    ma, count = lax.axis_index("ma"), lax.axis_size("ma")
    peers = [lax.rem(ma + step, count) for step in range(1, count)]
    greet(peers)
    swaps = []
    for i, peer in enumerate(peers):
        swaps.append(
            pltpu.make_async_remote_copy(
                src_ref=partial,
                dst_ref=other.at[i],
                send_sem=send.at[i],
                recv_sem=recv.at[i],
                device_id={"ma": peer},
                device_id_type=MESH,
            )
        )
        swaps[-1].start()

    def iota(shape, dim):
        return lax.broadcasted_iota(jnp.int32, shape, dim)

    def along(own, before, after, width):
        size = own.shape[1]
        return jnp.concatenate(
            [own[0:2], before[0:2, size - width : size], after[0:2, 0:width]], axis=1
        )

    lat_all = along(lat, lat_low, lat_high, FR)
    lon_all = along(lon, lon_west, lon_east, FC)
    lat_at = lat_all[0:1] - (lax.axis_index("gy") * rows).astype(F32)
    lat_w = lat_all[1:2]
    lon_total = float(cols * lax.axis_size("gx"))
    lon_at = lon_all[0:1] - (lax.axis_index("gx") * cols).astype(F32)
    lon_at = jnp.where(
        lon_at < -64.0, lon_at + lon_total, jnp.where(lon_at >= lon_total - 64.0, lon_at - lon_total, lon_at)
    )
    lon_w = lon_all[1:2]
    up_lat = weigh(place(iota((rows + 2 * CR, tall), 0), rows, CR), lat_at, lat_w)
    down_lat = weigh(place(iota((rows + 2 * HB, tall), 0), rows, HB), lat_at, lat_w)

    for copy in swaps:
        copy.wait_recv()
    for l in range(levels):
        total = partial[l]
        for i in range(count - 1):
            total = total + other[i, l]
        cells[l] = total
        mine[:, 2 * l * FC : (2 * l + 1) * FC] = total[:, :FC]
        mine[:, (2 * l + 1) * FC : (2 * l + 2) * FC] = total[:, cols - FC :]
    base = count - 1
    sides = [
        Link("gx", 1, mine, cells.at[levels], send, recv, base, True),
        Link("gx", -1, mine, cells.at[levels + 1], send, recv, base + 1, True),
    ]
    for one in sides:
        one.start()
    for one in sides:
        one.arrive()
    edge[0] = cells[:, rows - CR :, :]
    edge[1] = cells[:, :CR, :]
    ends = [
        Link("gy", 1, edge.at[0], low, send, recv, base + 2, False),
        Link("gy", -1, edge.at[1], high, send, recv, base + 3, False),
    ]
    for one in ends:
        one.start()
    for one in ends:
        one.arrive()

    def framed(i):
        return jnp.concatenate([cells[i], low[i], high[i]], axis=0)

    wings = [framed(levels), framed(levels + 1)]

    def fine_of(i, core, l):
        off = (i * levels + l) * FC
        body_rows = jnp.concatenate([core[l], fine_low[i, l], fine_high[i, l]], axis=0)
        return jnp.concatenate(
            [body_rows, fine_west[:, off : off + FC], fine_east[:, off : off + FC]], axis=1
        )

    for l in range(levels):
        order = iota((cols + 4 * levels * FC, wide), 0)
        j = order - cols
        lane = j % (2 * FC)
        whose = (j % (2 * levels * FC)) // (2 * FC) == l
        west = j < 2 * levels * FC
        pos = jnp.where(west, lane - 2 * FC, cols + lane)
        good = whose & ((west & (lane >= FC)) | ((j >= 2 * levels * FC) & (lane < FC)))
        pos = jnp.where(order < cols, order, jnp.where(good, pos, -1000))
        up_lon = weigh(pos, lon_at, lon_w)
        wide_cells = jnp.concatenate([framed(l)] + wings, axis=1)
        inc = across(up_lat, exact_dot(wide_cells, up_lon), (0, 0))
        increment[l] = inc[:frows, :fcols]
        misfit = fine_of(1, weight, l) * (inc - fine_of(0, innov, l))
        order = iota((cols + 2 * half, wide), 0)
        q = order - cols
        pos = jnp.where(q // half == l, q % HB - HB, cols + q % HB)
        down_lon = weigh(jnp.where(order < cols, order, pos), lon_at, lon_w)
        residual[l] = exact_dot(down_lat, across(misfit, down_lon, (1, 1)))
    for copy in swaps:
        copy.wait_send()
    for one in sides + ends:
        one.sent()


def fine_step(partial, innov, weight, fine_halos, lat, lat_halos, lon, lon_halos):
    levels, rows, cols = partial.shape
    others = lax.axis_size("ma") - 1
    vmem = pl.BlockSpec(memory_space=pltpu.VMEM)
    return pl.pallas_call(
        fine_kernel,
        in_specs=[vmem] * 13,
        out_specs=[vmem] * 2,
        out_shape=[
            jax.ShapeDtypeStruct(innov.shape, F32),
            jax.ShapeDtypeStruct((levels, rows + 2 * HB, cols + 2 * GROUP * HB), F32),
        ],
        scratch_shapes=[
            pltpu.VMEM((rows, 2 * levels * FC), F32),
            pltpu.VMEM((others, levels, rows, cols), F32),
            pltpu.VMEM((levels + 2, rows, cols), F32),
            pltpu.VMEM((2, levels + 2, CR, cols), F32),
            pltpu.VMEM((levels + 2, CR, cols), F32),
            pltpu.VMEM((levels + 2, CR, cols), F32),
            pltpu.SemaphoreType.DMA((others + 4,)),
            pltpu.SemaphoreType.DMA((others + 4,)),
        ],
        compiler_params=pltpu.CompilerParams(
            collective_id=1, has_side_effects=True, vmem_limit_bytes=VMEM_LIMIT
        ),
        cost_estimate=cost(2**29, 2**21),
    )(partial, innov, weight, *fine_halos, lat, *lat_halos, lon, *lon_halos)


def body(
    alpha_fields,
    member_perts,
    band_widths,
    lat_index,
    lat_weight,
    lon_index,
    lon_weight,
    innovation,
    obs_weight,
):
    rows, cols = alpha_fields.shape[2:]
    lon, lat = filter_matrices(band_widths, rows, cols)
    def table(index, weight):
        blank = jnp.zeros((6,) + index.shape, F32)
        return jnp.concatenate([index.astype(F32)[None], weight[None], blank])

    lat_data, lon_data = table(lat_index, lat_weight), table(lon_index, lon_weight)
    halos = exchange(alpha_fields, member_perts, innovation, obs_weight, lat_data, lon_data)
    a_north, a_south, a_west, a_east, p_north, p_south, p_west, p_east = halos[:8]
    partial = forward(alpha_fields, a_north, a_south, a_west, a_east, member_perts, lon, lat)
    increment, residual = fine_step(
        partial, innovation, obs_weight, halos[8:12], lat_data, halos[12:14], lon_data, halos[14:16]
    )
    gradient = adjoint(
        alpha_fields, member_perts, p_north, p_south, p_west, p_east, residual, lon, lat
    )
    return (increment, gradient)


def solution(mesh):
    placed = (
        P("ma", None, "gy", "gx"),
        P("ma", None, "gy", "gx"),
        P(),
        P("gy"),
        P("gy"),
        P("gx"),
        P("gx"),
        P(None, "gy", "gx"),
        P(None, "gy", "gx"),
    )
    return jax.shard_map(
        body,
        mesh=mesh,
        in_specs=placed,
        out_specs=(P(None, "gy", "gx"), P("ma", None, "gy", "gx")),
        check_vma=False,
    )
```
